32 devices in a mesh: dp: 8 (over y, x, core), mp: 4 (over z).
Axes of the slice: x: 2, y: 2, z: 4, core: 2. Of those that a mesh axis runs over, the one named last changes fastest.
Arguments:
- hidden_rows: bfloat16 [4096, 3584], P('dp'), may hold values from -6 to 6
- key_grad: bfloat16 [4096, 512], P('dp', 'mp'), may hold values from -6 to 6
- value_grad: bfloat16 [4096, 512], P('dp', 'mp'), may hold values from -6 to 6
- visual_rows: bfloat16 [2048, 1024], P('dp'), may hold values from -6 to 6
- visual_cotangent: bfloat16 [8, 4, 64, 3584], P('dp'), may hold values from -6 to 6
- norm_gain: float32 [1024], replicated, may hold values from 0.25 to 1.75
- norm_bias: float32 [1024], replicated, may hold values from -3 to 3
- fc1_weight: bfloat16 [1024, 4096], P(None, 'mp'), may hold values from -0.1875 to 0.1875
- fc1_bias: float32 [4096], P('mp'), may hold values from -3 to 3
- fc2_weight: bfloat16 [4096, 1024], P('mp'), may hold values from -0.09375 to 0.09375
- fc2_bias: float32 [1024], replicated, may hold values from -3 to 3
- layer_scale: float32 [1024], replicated, may hold values from 0.3 to 1.5
- token_counts: int32 [8, 8], P('dp'), may hold values from 1 to 32, as said below
- dest_offsets: int32 [8, 8], P('dp'), may hold values from 1 to 4, as said below
Outputs:
- key_weight_grad: float32 [3592, 512], P('dp', 'mp')
- value_weight_grad: float32 [3592, 512], P('dp', 'mp')
- projector_grad: float32 [3592, 1024], P('dp', 'mp')
- handoff: bfloat16 [8, 4, 64, 1024], P('dp', None, None, 'mp')
The draws below stay inside these ranges and needn't reach their ends.
Inputs may be any that keep to these rules, and one draw needn't show every extreme that they name: `token_counts`: on every data rank the images of one distance, chosen per rank, all have 32 rows. `dest_offsets`: every data rank sends exactly 2 images to each distance from 1 to 4.
All inputs are finite; a program needn't handle non-finite values.
Results may differ from the reference program's by a relative error of at most 0.0046.
Values may be sent and summed in bfloat16 or wider, within the bound.
No kernel may reach another device: no remote copies, remote signals or barrier semaphores. Data moves between devices by JAX's collectives and lax.ppermute only.
A program may use at most 64 MiB of HBM per device.

```python
import math
import jax
import jax.numpy as jnp
from jax import lax

D = 3584
KV_WIDTH = 512
FEAT = 1024
MLP = 4096
TOK_DEV = 512
MOST_TOK = 32
SPREAD = 4
IMG_DEV = 8
ROWS_DEV = 256
CAP = 64
TOKENS = 4096
D_PAD = 3592
N_DP = 8


def routing_table(key):
    base = jax.random.fold_in(key, 11)
    source_keys = jax.random.split(base, N_DP)

    def one_source(source_key):
        first, second, third = jax.random.split(source_key, 3)
        order = jax.random.permutation(first, IMG_DEV)
        offsets = (order % SPREAD + 1).astype(jnp.int32)
        counts = jax.random.randint(second, (IMG_DEV,), 1, MOST_TOK + 1).astype(jnp.int32)
        filled = jax.random.randint(third, (), 1, SPREAD + 1).astype(jnp.int32)
        counts = jnp.where(offsets == filled, MOST_TOK, counts).astype(jnp.int32)
        return (counts, offsets)
    return jax.vmap(one_source)(source_keys)


def draw_token_counts(key, part):
    return routing_table(key)[0]


def draw_dest_offsets(key, part):
    return routing_table(key)[1]


def strengthened(values, own_key, source, target, shards_of, factor):
    owner, partner = [(jnp.arange(values.shape[dim]) // (values.shape[dim] // shards_of)).reshape([-1 if axis == dim else 1 for axis in range(values.ndim)]) for dim in (source, target)]
    chosen = jax.random.permutation(own_key, shards_of)[partner]
    strong = (owner == chosen) | (owner == (partner + shards_of // 2) % shards_of)
    return jnp.where(strong, factor * values, values)


def block_levels(key, shape, shards, smallest, high):
    loudness = 1.0
    for dim, blocks in shards:
        draws = jax.random.uniform(jax.random.fold_in(jax.random.fold_in(key, 6), dim), (blocks,), jnp.float32, smallest / len(shards), high / len(shards))
        loudness = loudness * jnp.repeat(jnp.exp(draws), shape[dim] // blocks).reshape((-1,) + (1,) * (len(shape) - 1 - dim))
    return loudness


def noise(own_key, shape, scale, reach, cuts=(), dtype=jnp.bfloat16):
    result = scale * jax.random.normal(own_key, shape, jnp.float32)
    if cuts:
        result = result * block_levels(own_key, shape, cuts, -0.22, 0.18)
    return jnp.clip(result, -reach, reach).astype(dtype)


def noise_with(stream_key, shape, spread, bound, cuts, heavy, dtype=jnp.bfloat16):
    entries = spread * jax.random.normal(stream_key, shape, jnp.float32)
    if cuts:
        entries = entries * block_levels(stream_key, shape, cuts, -0.22, 0.18)
    return jnp.clip(strengthened(entries, jax.random.fold_in(stream_key, 3), *heavy), -bound, bound).astype(dtype)


def setup_inputs(seed: int = 0) -> dict:
    keys = jax.random.split(jax.random.key(seed), 15)
    return {
        "hidden_rows": noise_with(keys[0], (TOKENS, D), 1.0, 6.0, ((0, 8),), (0, 1, 8, 2.0)),
        "key_grad": noise(keys[1], (TOKENS, KV_WIDTH), 1.0, 6.0, ((0, 8), (1, 4))),
        "value_grad": noise(keys[2], (TOKENS, KV_WIDTH), 1.0, 6.0, ((0, 8), (1, 4))),
        "visual_rows": noise(keys[3], (N_DP * ROWS_DEV, FEAT), 1.0, 6.0, ((0, 8),)),
        "visual_cotangent": noise_with(keys[4], (N_DP, SPREAD, CAP, D), 1.0, 6.0, ((0, 8),), (0, 3, 8, 2.0)),
        "norm_gain": jnp.clip(1.0 + 0.15 * jax.random.normal(keys[5], (FEAT,), jnp.float32), 0.25, 1.75),
        "norm_bias": noise(keys[6], (FEAT,), 0.5, 3.0, (), jnp.float32),
        "fc1_weight": noise(keys[7], (FEAT, MLP), FEAT ** -0.5, 0.1875, ((1, 4),)),
        "fc1_bias": noise(keys[8], (MLP,), 0.5, 3.0, ((0, 4),), jnp.float32),
        "fc2_weight": noise(keys[9], (MLP, FEAT), MLP ** -0.5, 0.09375, ((0, 4),)),
        "fc2_bias": noise(keys[10], (FEAT,), 0.5, 3.0, (), jnp.float32),
        "layer_scale": jnp.clip(jnp.exp(jax.random.uniform(keys[11], (FEAT,), jnp.float32, math.log(0.3), math.log(1.5))), 0.3, 1.5),
        "token_counts": draw_token_counts(jax.random.fold_in(keys[14], 71), 0),
        "dest_offsets": draw_dest_offsets(jax.random.fold_in(keys[14], 71), 0),
    }


def pack_rows(rows, counts, offsets):
    total_rows = rows.shape[0]
    images = counts.shape[0]
    counts = counts.astype(jnp.int32)
    offsets = offsets.astype(jnp.int32)
    ends = jnp.cumsum(counts).astype(jnp.int32)
    starts = (ends - counts).astype(jnp.int32)
    places = jnp.arange(total_rows).astype(jnp.int32)
    image_ids = jnp.arange(images).astype(jnp.int32)
    owner = lax.optimization_barrier(jnp.sum((places[:, None] >= ends[None, :]).astype(jnp.int32), axis=1)).astype(jnp.int32)
    member = (owner[:, None] == image_ids[None, :]).astype(jnp.int32)
    earlier = (image_ids[None, :] < image_ids[:, None]) & (offsets[None, :] == offsets[:, None])
    before = lax.optimization_barrier(jnp.sum(earlier.astype(jnp.int32) * counts[None, :], axis=1)).astype(jnp.int32)
    row_dest = lax.optimization_barrier(jnp.sum(member * offsets[None, :], axis=1)).astype(jnp.int32)
    row_start = lax.optimization_barrier(jnp.sum(member * starts[None, :], axis=1)).astype(jnp.int32)
    row_before = lax.optimization_barrier(jnp.sum(member * before[None, :], axis=1)).astype(jnp.int32)
    slot_index = row_before + places - row_start
    target = jnp.where(places < ends[images - 1], (row_dest - 1) * CAP + slot_index, -1).astype(jnp.int32)
    slot_ids = jnp.arange(SPREAD * CAP).astype(jnp.int32)
    select = (slot_ids[:, None] == target[None, :]).astype(jnp.bfloat16)
    packed = jnp.dot(select, rows, preferred_element_type=jnp.float32).astype(jnp.bfloat16)
    return packed.reshape(SPREAD, CAP, rows.shape[1])

def encode(rows, norm_gain, norm_bias, fc1_weight, fc1_bias, fc2_weight, fc2_bias, layer_scale):
    values = rows.astype(jnp.float32)
    center = lax.optimization_barrier(jnp.mean(values, axis=1, keepdims=True))
    spread_sq = lax.optimization_barrier(jnp.mean((values - center) ** 2, axis=1, keepdims=True))
    normed = ((values - center) * lax.rsqrt(spread_sq + 1e-06) * norm_gain + norm_bias).astype(jnp.bfloat16)
    hidden = jax.nn.gelu(jnp.dot(normed, fc1_weight, preferred_element_type=jnp.float32) + fc1_bias, approximate=False).astype(jnp.bfloat16)
    partial_value = jnp.dot(hidden, fc2_weight, preferred_element_type=jnp.float32)
    return (values + layer_scale * (partial_value + fc2_bias)).astype(jnp.bfloat16)

def reference(hidden_rows, key_grad, value_grad, visual_rows, visual_cotangent, norm_gain, norm_bias, fc1_weight, fc1_bias, fc2_weight, fc2_bias, layer_scale, token_counts, dest_offsets):
    width = hidden_rows.shape[1]
    blocks = hidden_rows.reshape(N_DP, TOK_DEV, width)
    key_blocks = key_grad.reshape(N_DP, TOK_DEV, KV_WIDTH)
    value_blocks = value_grad.reshape(N_DP, TOK_DEV, KV_WIDTH)

    def accumulate(carry, pieces):
        inputs, key_piece, value_piece = pieces
        key_total, value_total = carry
        key_total = key_total + lax.dot_general(inputs, key_piece, (((0,), (0,)), ((), ())), preferred_element_type=jnp.float32)
        value_total = value_total + lax.dot_general(inputs, value_piece, (((0,), (0,)), ((), ())), preferred_element_type=jnp.float32)
        return ((key_total, value_total), None)
    empty = jnp.zeros((width, KV_WIDTH), jnp.float32)
    (key_total, value_total), _ = lax.scan(accumulate, (empty, empty), (blocks, key_blocks, value_blocks))
    key_bias = lax.optimization_barrier(jnp.sum(key_grad.astype(jnp.float32), axis=0))[None, :]
    value_bias = lax.optimization_barrier(jnp.sum(value_grad.astype(jnp.float32), axis=0))[None, :]
    zero_rows = jnp.zeros((D_PAD - width - 1, KV_WIDTH), jnp.float32)
    key_weight_grad = jnp.concatenate([key_total, key_bias, zero_rows], axis=0)
    value_weight_grad = jnp.concatenate([value_total, value_bias, zero_rows], axis=0)
    encoded = encode(visual_rows, norm_gain, norm_bias, fc1_weight, fc1_bias, fc2_weight, fc2_bias, layer_scale)
    packed = jax.vmap(pack_rows)(encoded.reshape(N_DP, ROWS_DEV, FEAT), token_counts, dest_offsets)
    handoff = jnp.stack([jnp.roll(packed[:, distance], distance + 1, axis=0) for distance in range(SPREAD)], axis=1)
    cot_flat = visual_cotangent.reshape(N_DP * SPREAD * CAP, width)
    rows_flat = handoff.reshape(N_DP * SPREAD * CAP, FEAT)
    projector_main = lax.dot_general(cot_flat, rows_flat, (((0,), (0,)), ((), ())), preferred_element_type=jnp.float32)
    projector_grad = jnp.concatenate([projector_main, jnp.zeros((D_PAD - width, FEAT), jnp.float32)], axis=0)
    return (key_weight_grad, value_weight_grad, projector_grad, handoff)
```

```python
from functools import partial

import jax
import jax.numpy as jnp
from jax import lax
from jax.experimental import pallas as pl
from jax.experimental.pallas import tpu as pltpu
from jax.sharding import PartitionSpec as P

SPREAD = 4
CAP = 64
FEW = 8
CHUNK = 512


def chip_shift(x, by):
    count = lax.axis_size("dp")
    return lax.ppermute(x, "dp", [(i, (i + 2 * by) % count) for i in range(count)])


def core_swap(x):
    count = lax.axis_size("dp")
    return lax.ppermute(x, "dp", [(i, i ^ 1) for i in range(count)])


def partial_kernel(core_ref, left_ref, right_ref, keep_ref, send_ref, total_ref, *, ranks, rows, width, ones_row):
    step = pl.program_id(0)
    chunk = left_ref.shape[1]
    right = right_ref[...]
    total_ref[pl.ds(pl.multiple_of(step * chunk, 8), chunk), :] = lax.dot_general(
        left_ref[...], right, (((0,), (0,)), ((), ())), preferred_element_type=jnp.float32
    )

    @pl.when(step == pl.num_programs(0) - 1)
    def _():
        extra = total_ref.shape[0] - width
        if ones_row:
            first = lax.broadcasted_iota(jnp.int32, (extra, right.shape[0]), 0) == 0
            picked = jnp.where(first, 1.0, 0.0).astype(jnp.bfloat16)
            total_ref[width:, :] = jnp.dot(picked, right, preferred_element_type=jnp.float32)
        else:
            total_ref[width:, :] = jnp.zeros((extra, right.shape[1]), jnp.float32)
        for core in range(2):

            @pl.when(core_ref[0] == core)
            def _():
                for rank in range(ranks):
                    piece = total_ref[rank * rows : (rank + 1) * rows, :].astype(jnp.bfloat16)
                    if rank % 2 == core:
                        keep_ref[rank // 2] = piece
                    else:
                        send_ref[rank // 2] = piece


def partial_blocks(left, right, ranks, rows, ones_row):
    tokens, width = left.shape
    cols = right.shape[1]
    chunk = CHUNK if width % CHUNK == 0 else width
    core = jnp.reshape(lax.axis_index("dp") % 2, (1,)).astype(jnp.int32)
    block = jax.ShapeDtypeStruct((ranks // 2, rows, cols), jnp.bfloat16)
    whole = pl.BlockSpec((ranks // 2, rows, cols), lambda i, s: (0, 0, 0))
    return pl.pallas_call(
        partial(partial_kernel, ranks=ranks, rows=rows, width=width, ones_row=ones_row),
        out_shape=(block, block),
        grid_spec=pltpu.PrefetchScalarGridSpec(
            num_scalar_prefetch=1,
            grid=(width // chunk,),
            in_specs=[
                pl.BlockSpec((tokens, chunk), lambda i, s: (0, i)),
                pl.BlockSpec((tokens, cols), lambda i, s: (0, 0)),
            ],
            out_specs=(whole, whole),
            scratch_shapes=[pltpu.VMEM((ranks * rows, cols), jnp.float32)],
        ),
        name="partial_kv" if ones_row else "partial_proj",
    )(core, left, right)


def chip_sum_kernel(chip_ref, keep_ref, got_ref, own_ref, *send_refs):
    chips = keep_ref.shape[0]
    for distance in range(chips):
        target = lax.rem(chip_ref[0] + distance, chips)
        total = keep_ref[target].astype(jnp.float32) + got_ref[target].astype(jnp.float32)
        if distance == 0:
            own_ref[...] = total
        else:
            send_refs[distance - 1][...] = total.astype(jnp.bfloat16)


def chip_sums(keep, got, name):
    chips, rows, cols = keep.shape
    chip = jnp.reshape(lax.axis_index("dp") // 2, (1,)).astype(jnp.int32)
    return pl.pallas_call(
        chip_sum_kernel,
        in_specs=[
            pl.BlockSpec(memory_space=pltpu.SMEM),
            pl.BlockSpec(memory_space=pltpu.VMEM),
            pl.BlockSpec(memory_space=pltpu.VMEM),
        ],
        out_shape=(jax.ShapeDtypeStruct((rows, cols), jnp.float32),)
        + (jax.ShapeDtypeStruct((rows, cols), jnp.bfloat16),) * (chips - 1),
        name=name,
    )(chip, keep, got)


def reduced_rows(left, right, ranks, rows, ones_row):
    if ranks <= FEW and ranks % 2 == 0:
        keep, send = partial_blocks(left, right, ranks, rows, ones_row)
        got = core_swap(send)
        own, *sends = chip_sums(keep, got, "chip_kv" if ones_row else "chip_proj")
        total = own
        for distance, block in enumerate(sends, 1):
            total = total + chip_shift(block, distance).astype(jnp.float32)
        return total
    tokens, width = left.shape
    filler = jnp.zeros((tokens, ranks * rows - width), jnp.bfloat16)
    if ones_row:
        filler = filler.at[:, 0].set(1)
    padded = jnp.concatenate([left, filler], axis=1)
    product = lax.dot_general(padded, right, (((0,), (0,)), ((), ())), preferred_element_type=jnp.float32)
    return lax.psum_scatter(product, "dp", scatter_dimension=0, tiled=True)


def feature_sum(value):
    shards = lax.axis_size("mp")
    rows, width = value.shape
    cols = width // shards
    if shards > FEW:
        return lax.psum_scatter(value, "mp", scatter_dimension=1, tiled=True)
    me = lax.axis_index("mp")
    total = lax.dynamic_slice_in_dim(value, me * cols, cols, 1)
    narrow = value.astype(jnp.bfloat16)
    for distance in range(1, shards):
        piece = lax.dynamic_slice_in_dim(narrow, ((me + distance) % shards) * cols, cols, 1)
        total = total + shifted(piece, "mp", distance).astype(jnp.float32)
    return total


def shifted(x, axis, by):
    count = lax.axis_size(axis)
    return lax.ppermute(x, axis, [(i, (i + by) % count) for i in range(count)])


def pack_rows(rows, counts, offsets):
    total_rows = rows.shape[0]
    images = counts.shape[0]
    ends = jnp.cumsum(counts)
    starts = ends - counts
    places = jnp.arange(total_rows)
    image_ids = jnp.arange(images)
    owner = jnp.sum((places[:, None] >= ends[None, :]).astype(jnp.int32), axis=1)
    member = (owner[:, None] == image_ids[None, :]).astype(jnp.int32)
    earlier = (image_ids[None, :] < image_ids[:, None]) & (offsets[None, :] == offsets[:, None])
    before = jnp.sum(earlier.astype(jnp.int32) * counts[None, :], axis=1)
    row_dest = jnp.sum(member * offsets[None, :], axis=1)
    row_start = jnp.sum(member * starts[None, :], axis=1)
    row_before = jnp.sum(member * before[None, :], axis=1)
    slot_index = row_before + places - row_start
    target = jnp.where(places < ends[images - 1], (row_dest - 1) * CAP + slot_index, -1)
    slot_ids = jnp.arange(SPREAD * CAP)
    select = (slot_ids[:, None] == target[None, :]).astype(jnp.bfloat16)
    packed = jnp.dot(select, rows, preferred_element_type=jnp.float32).astype(jnp.bfloat16)
    return packed.reshape(SPREAD, CAP, rows.shape[1])


def vision(
    visual_rows,
    norm_gain,
    norm_bias,
    fc1_weight,
    fc1_bias,
    fc2_weight,
    fc2_bias,
    layer_scale,
    token_counts,
    dest_offsets,
):
    values = visual_rows.astype(jnp.float32)
    center = jnp.mean(values, axis=1, keepdims=True)
    spread_sq = jnp.mean((values - center) ** 2, axis=1, keepdims=True)
    normed = ((values - center) * lax.rsqrt(spread_sq + 1e-06) * norm_gain + norm_bias).astype(
        jnp.bfloat16
    )
    hidden = jax.nn.gelu(
        jnp.dot(normed, fc1_weight, preferred_element_type=jnp.float32) + fc1_bias,
        approximate=False,
    ).astype(jnp.bfloat16)
    partial_value = jnp.dot(hidden, fc2_weight, preferred_element_type=jnp.float32)
    summed = feature_sum(partial_value)
    column_count = summed.shape[1]
    first_col = lax.axis_index("mp") * column_count
    own_values = lax.dynamic_slice_in_dim(values, first_col, column_count, 1)
    own_scale = lax.dynamic_slice_in_dim(layer_scale, first_col, column_count, 0)
    own_bias = lax.dynamic_slice_in_dim(fc2_bias, first_col, column_count, 0)
    encoded = (own_values + own_scale * (summed + own_bias)).astype(jnp.bfloat16)
    packed = pack_rows(encoded, token_counts[0], dest_offsets[0])
    received = []
    for distance in range(SPREAD):
        received.append(shifted(packed[distance], "dp", distance + 1))
    return jnp.stack(received, axis=0)[None]


def per_device(
    hidden_rows,
    key_grad,
    value_grad,
    visual_rows,
    visual_cotangent,
    norm_gain,
    norm_bias,
    fc1_weight,
    fc1_bias,
    fc2_weight,
    fc2_bias,
    layer_scale,
    token_counts,
    dest_offsets,
):
    width = hidden_rows.shape[1]
    devices = lax.axis_size("dp")
    shard_rows = (width + devices) // devices
    key_cols = key_grad.shape[1]
    kv_cotangent = jnp.concatenate([key_grad, value_grad], axis=1)
    kv_results = reduced_rows(hidden_rows, kv_cotangent, devices, shard_rows, True)
    key_weight_grad = kv_results[:, :key_cols]
    value_weight_grad = kv_results[:, key_cols:]
    handoff = vision(
        visual_rows,
        norm_gain,
        norm_bias,
        fc1_weight,
        fc1_bias,
        fc2_weight,
        fc2_bias,
        layer_scale,
        token_counts,
        dest_offsets,
    )
    slot_count = handoff.shape[1] * handoff.shape[2]
    cotangent = visual_cotangent.reshape(slot_count, width)
    received_rows = handoff.reshape(slot_count, handoff.shape[3])
    projector_grad = reduced_rows(cotangent, received_rows, devices, shard_rows, False)
    return (key_weight_grad, value_weight_grad, projector_grad, handoff)


def solution(mesh):
    placed = (
        P("dp", None),
        P("dp", "mp"),
        P("dp", "mp"),
        P("dp", None),
        P("dp", None, None, None),
        P(),
        P(),
        P(None, "mp"),
        P("mp"),
        P("mp", None),
        P(),
        P(),
        P("dp", None),
        P("dp", None),
    )
    return jax.shard_map(
        per_device,
        mesh=mesh,
        in_specs=placed,
        out_specs=(P("dp", "mp"), P("dp", "mp"), P("dp", "mp"), P("dp", None, None, "mp")),
        check_vma=False,
    )
```

```python
from functools import partial

import jax
import jax.numpy as jnp
from jax import lax
from jax.experimental import pallas as pl
from jax.experimental.pallas import tpu as pltpu
from jax.sharding import PartitionSpec as P

FEW = 8
CHUNK = 512
ANY = pl.BlockSpec(memory_space=pl.ANY)
VMEM = pl.BlockSpec(memory_space=pltpu.VMEM)
SMEM = pl.BlockSpec(memory_space=pltpu.SMEM)


def shifted(x, axis, by):
    count = lax.axis_size(axis)
    return lax.ppermute(x, axis, [(i, (i + by) % count) for i in range(count)])


def core_swap(x):
    count = lax.axis_size("dp")
    return lax.ppermute(x, "dp", [(i, i ^ 1) for i in range(count)])


def scalar(value):
    return jnp.reshape(value, (1,)).astype(jnp.int32)


def padded(rows):
    return (rows + 15) // 16 * 16


def partial_kernel(core_ref, left_hbm, *refs, parts, ranks, rows, ones_row):
    rights = refs[:parts]
    keep_hbm, send_hbm, left, right_ref, total, stage, in_sem, out_sem = refs[parts:]
    chunks, tokens, chunk = left.shape
    width = chunks * chunk
    stride = stage.shape[1]
    incoming = [
        pltpu.make_async_copy(left_hbm.at[:, pl.ds(c * chunk, chunk)], left.at[c], in_sem.at[c])
        for c in range(chunks)
    ]
    for copy in incoming:
        copy.start()
    if ones_row:
        right = jnp.concatenate([part[...] for part in rights], axis=1)
    else:
        right = jnp.concatenate([part[...] for part in rights], axis=0)
    right_ref[...] = right
    extra = total.shape[0] - width
    if ones_row:
        first = lax.broadcasted_iota(jnp.int32, (extra, tokens), 0) == 0
        picked = jnp.where(first, 1.0, 0.0).astype(jnp.bfloat16)
        total[width:, :] = jnp.dot(picked, right_ref[...], preferred_element_type=jnp.float32)
    else:
        total[width:, :] = jnp.zeros((extra, total.shape[1]), jnp.float32)
    tail = rows // 16 * 16
    if tail < rows:
        for rank in range(ranks):
            stage[rank, tail:, :] = jnp.zeros((stride - tail, total.shape[1]), jnp.bfloat16)

    def outgoing(rank, target):
        place = pl.ds(rank // 2 * stride, stride)
        return pltpu.make_async_copy(stage.at[rank], target.at[place, :], out_sem.at[rank])

    rank = 0
    for c in range(chunks):
        incoming[c].wait()
        total[c * chunk : (c + 1) * chunk, :] = lax.dot_general(
            left[c], right_ref[...], (((0,), (0,)), ((), ())), preferred_element_type=jnp.float32
        )
        ready = (c + 1) * chunk if c + 1 < chunks else ranks * rows
        while rank < ranks and (rank + 1) * rows <= ready:
            stage[rank, :rows, :] = total[rank * rows : (rank + 1) * rows, :].astype(jnp.bfloat16)

            @pl.when(core_ref[0] == rank % 2)
            def _(rank=rank):
                outgoing(rank, keep_hbm).start()

            @pl.when(core_ref[0] != rank % 2)
            def _(rank=rank):
                outgoing(rank, send_hbm).start()

            rank += 1
    for rank in range(ranks):
        outgoing(rank, keep_hbm).wait()


def partial_blocks(left, rights, ranks, rows, ones_row):
    tokens, width = left.shape
    cols = sum(part.shape[1] for part in rights) if ones_row else rights[0].shape[1]
    chunk = CHUNK if width % CHUNK == 0 else width
    stride = padded(rows)
    block = jax.ShapeDtypeStruct((ranks // 2 * stride, cols), jnp.bfloat16)
    return pl.pallas_call(
        partial(partial_kernel, parts=len(rights), ranks=ranks, rows=rows, ones_row=ones_row),
        out_shape=(block, block),
        in_specs=[SMEM, ANY] + [VMEM] * len(rights),
        out_specs=(ANY, ANY),
        scratch_shapes=[
            pltpu.VMEM((width // chunk, tokens, chunk), jnp.bfloat16),
            pltpu.VMEM((tokens, cols), jnp.bfloat16),
            pltpu.VMEM((ranks * rows, cols), jnp.float32),
            pltpu.VMEM((ranks, stride, cols), jnp.bfloat16),
            pltpu.SemaphoreType.DMA((width // chunk,)),
            pltpu.SemaphoreType.DMA((ranks,)),
        ],
        name="partial_kv" if ones_row else "partial_proj",
    )(scalar(lax.axis_index("dp") % 2), left, *rights)


def chip_sum_kernel(chip_ref, keep_hbm, got_hbm, *refs):
    chips = (len(refs) - 5) if len(refs) > 5 else 1
    outs = refs[:chips]
    keep, got, stage, in_sem, out_sem = refs[chips:]
    stride = keep.shape[1]
    rows = outs[0].shape[0]
    order = list(range(1, chips)) + [0]
    copies = {}
    for distance in order:
        target = lax.rem(chip_ref[0] + distance, chips)
        place = pl.ds(pl.multiple_of(target * stride, 16), stride)
        copies[distance] = (
            pltpu.make_async_copy(keep_hbm.at[place, :], keep.at[distance], in_sem.at[distance, 0]),
            pltpu.make_async_copy(got_hbm.at[place, :], got.at[distance], in_sem.at[distance, 1]),
        )
        for copy in copies[distance]:
            copy.start()
    leaving = []
    for distance in order:
        for copy in copies[distance]:
            copy.wait()
        total = keep[distance].astype(jnp.float32) + got[distance].astype(jnp.float32)
        if distance == 0:
            outs[0][...] = total[:rows, :]
        else:
            stage[distance - 1] = total.astype(jnp.bfloat16)
            leaving.append(
                pltpu.make_async_copy(stage.at[distance - 1], outs[distance], out_sem.at[distance - 1])
            )
            leaving[-1].start()
    for copy in leaving:
        copy.wait()


def chip_sums(keep, got, chips, rows, name):
    stride, cols = keep.shape[0] // chips, keep.shape[1]
    return pl.pallas_call(
        chip_sum_kernel,
        in_specs=[SMEM, ANY, ANY],
        out_specs=(VMEM,) + (ANY,) * (chips - 1),
        out_shape=(jax.ShapeDtypeStruct((rows, cols), jnp.float32),)
        + (jax.ShapeDtypeStruct((stride, cols), jnp.bfloat16),) * (chips - 1),
        scratch_shapes=[
            pltpu.VMEM((chips, stride, cols), jnp.bfloat16),
            pltpu.VMEM((chips, stride, cols), jnp.bfloat16),
            pltpu.VMEM((max(chips - 1, 1), stride, cols), jnp.bfloat16),
            pltpu.SemaphoreType.DMA((chips, 2)),
            pltpu.SemaphoreType.DMA((max(chips - 1, 1),)),
        ],
        name=name,
    )(scalar(lax.axis_index("dp") // 2), keep, got)


def spread_sums(own, sends):
    rows = own.shape[0]
    total = own
    for distance, block in enumerate(sends, 1):
        total = total + shifted(block, "dp", 2 * distance)[:rows].astype(jnp.float32)
    return total


def plain_rows(left, right, ranks, rows, ones_row):
    tokens, width = left.shape
    filler = jnp.zeros((tokens, ranks * rows - width), jnp.bfloat16)
    if ones_row:
        filler = filler.at[:, 0].set(1)
    wide = jnp.concatenate([left, filler], axis=1)
    product = lax.dot_general(wide, right, (((0,), (0,)), ((), ())), preferred_element_type=jnp.float32)
    return lax.psum_scatter(product, "dp", scatter_dimension=0, tiled=True)


def encoder_kernel(me_ref, rows_ref, gain_ref, bias_ref, fc1_ref, b1_ref, fc2_ref, own_ref, *refs):
    sends = refs[:-2]
    normed, total = refs[-2:]
    shards, _, cols = total.shape
    step = pl.program_id(0)

    @pl.when(step == 0)
    def _():
        values = rows_ref[...].astype(jnp.float32)
        center = jnp.mean(values, axis=1, keepdims=True)
        moved = values - center
        spread_sq = jnp.mean(moved * moved, axis=1, keepdims=True)
        normed[...] = (moved * lax.rsqrt(spread_sq + 1e-06) * gain_ref[...] + bias_ref[...]).astype(
            jnp.bfloat16
        )

    before = jnp.dot(normed[...], fc1_ref[...], preferred_element_type=jnp.float32) + b1_ref[...]
    hidden = (0.5 * before * (1.0 + lax.erf(before * 0.7071067811865476))).astype(jnp.bfloat16)
    for shard in range(shards):
        piece = jnp.dot(
            hidden, fc2_ref[:, shard * cols : (shard + 1) * cols], preferred_element_type=jnp.float32
        )

        @pl.when(step == 0)
        def _(piece=piece, shard=shard):
            total[shard] = piece

        @pl.when(step > 0)
        def _(piece=piece, shard=shard):
            total[shard] += piece

    @pl.when(step == pl.num_programs(0) - 1)
    def _():
        own_ref[...] = total[me_ref[0]]
        for distance, send in enumerate(sends, 1):
            send[...] = total[lax.rem(me_ref[0] + distance, shards)].astype(jnp.bfloat16)


def encoder_partials(rows, gain, bias, fc1, b1, fc2):
    shards = lax.axis_size("mp")
    count, feats = rows.shape
    units = fc1.shape[1]
    chunk = 256 if units % 256 == 0 else units
    cols = feats // shards
    block = pl.BlockSpec((count, cols), lambda i, m: (0, 0))
    line = pl.BlockSpec((1, feats), lambda i, m: (0, 0))
    return pl.pallas_call(
        encoder_kernel,
        out_shape=(jax.ShapeDtypeStruct((count, cols), jnp.float32),)
        + (jax.ShapeDtypeStruct((count, cols), jnp.bfloat16),) * (shards - 1),
        grid_spec=pltpu.PrefetchScalarGridSpec(
            num_scalar_prefetch=1,
            grid=(units // chunk,),
            in_specs=[
                pl.BlockSpec((count, feats), lambda i, m: (0, 0)),
                line,
                line,
                pl.BlockSpec((feats, chunk), lambda i, m: (0, i)),
                pl.BlockSpec((1, chunk), lambda i, m: (0, i)),
                pl.BlockSpec((chunk, feats), lambda i, m: (i, 0)),
            ],
            out_specs=(block,) * shards,
            scratch_shapes=[
                pltpu.VMEM((count, feats), jnp.bfloat16),
                pltpu.VMEM((shards, count, cols), jnp.float32),
            ],
        ),
        name="encoder",
    )(scalar(lax.axis_index("mp")), rows, gain[None], bias[None], fc1, b1[None], fc2)


def pack_kernel(me_ref, counts_ref, offsets_ref, rows_ref, scale_ref, bias_ref, own_ref, *refs, spread):
    parts, outs = refs[:-spread], refs[-spread:]
    images = counts_ref.shape[0]
    cap = outs[0].shape[0]
    total_rows = rows_ref.shape[0]
    summed = own_ref[...]
    for part in parts:
        summed = summed + part[...].astype(jnp.float32)
    encoded = rows_ref[...].astype(jnp.float32) + scale_ref[...] * (summed + bias_ref[...])
    encoded = encoded.astype(jnp.bfloat16)
    place = lax.broadcasted_iota(jnp.int32, (1, total_rows), 1)
    target = jnp.full((1, total_rows), -1, jnp.int32)
    start = jnp.int32(0)
    for image in range(images):
        count, offset = counts_ref[image], offsets_ref[image]
        before = jnp.int32(0)
        for other in range(image):
            before = before + jnp.where(offsets_ref[other] == offset, counts_ref[other], 0)
        inside = (place >= start) & (place < start + count)
        target = jnp.where(inside, place + ((offset - 1) * cap + before - start), target)
        start = start + count
    slot = lax.broadcasted_iota(jnp.int32, (spread * cap, total_rows), 0)
    select = jnp.where(slot == target, 1.0, 0.0).astype(jnp.bfloat16)
    packed = jnp.dot(select, encoded, preferred_element_type=jnp.float32).astype(jnp.bfloat16)
    for distance in range(spread):
        outs[distance][...] = packed[distance * cap : (distance + 1) * cap, :]


def packed_rows(rows, scale, bias, own, parts, counts, offsets, spread, cap):
    count, cols = own.shape
    line = pl.BlockSpec((1, cols), lambda i, m, c, o: (0, m[0]))
    whole = pl.BlockSpec((count, cols), lambda i, m, c, o: (0, 0))
    return pl.pallas_call(
        partial(pack_kernel, spread=spread),
        out_shape=(jax.ShapeDtypeStruct((cap, cols), jnp.bfloat16),) * spread,
        grid_spec=pltpu.PrefetchScalarGridSpec(
            num_scalar_prefetch=3,
            grid=(1,),
            in_specs=[pl.BlockSpec((count, cols), lambda i, m, c, o: (0, m[0])), line, line]
            + [whole] * (1 + len(parts)),
            out_specs=(pl.BlockSpec((cap, cols), lambda i, m, c, o: (0, 0)),) * spread,
        ),
        name="pack",
    )(scalar(lax.axis_index("mp")), counts, offsets, rows, scale[None], bias[None], own, *parts)


def per_device(
    hidden_rows,
    key_grad,
    value_grad,
    visual_rows,
    visual_cotangent,
    norm_gain,
    norm_bias,
    fc1_weight,
    fc1_bias,
    fc2_weight,
    fc2_bias,
    layer_scale,
    token_counts,
    dest_offsets,
):
    width = hidden_rows.shape[1]
    ranks = lax.axis_size("dp")
    rows = (width + ranks) // ranks
    spread, cap = visual_cotangent.shape[1:3]
    key_cols = key_grad.shape[1]
    stepped = ranks <= FEW and ranks % 2 == 0
    chips = ranks // 2

    own, *sends = encoder_partials(
        visual_rows, norm_gain, norm_bias, fc1_weight, fc1_bias, fc2_weight
    )
    parts = [shifted(block, "mp", distance) for distance, block in enumerate(sends, 1)]
    if stepped:
        left, own = lax.optimization_barrier((hidden_rows, own))
        kv_keep, kv_send = partial_blocks(left, (key_grad, value_grad), ranks, rows, True)
        kv_got = core_swap(kv_send)
        own, kv_keep = lax.optimization_barrier((own, kv_keep))
    packed = packed_rows(
        visual_rows,
        layer_scale,
        fc2_bias,
        own,
        parts,
        token_counts[0],
        dest_offsets[0],
        spread,
        cap,
    )
    if stepped:
        packed, kv_keep = lax.optimization_barrier((packed, kv_keep))
    received = [shifted(block, "dp", distance) for distance, block in enumerate(packed, 1)]
    handoff = jnp.stack(received, axis=0)[None]
    cotangent = visual_cotangent.reshape(spread * cap, width)
    if stepped:
        kv_own, *kv_sends = chip_sums(kv_keep, kv_got, chips, rows, "chip_kv")
        cotangent, kv_own = lax.optimization_barrier((cotangent, kv_own))
        keep, send = partial_blocks(cotangent, received, ranks, rows, False)
        got = core_swap(send)
        kv_results = spread_sums(kv_own, kv_sends)
        proj_own, *proj_sends = chip_sums(keep, got, chips, rows, "chip_proj")
        projector_grad = spread_sums(proj_own, proj_sends)
    else:
        kv_cotangent = jnp.concatenate([key_grad, value_grad], axis=1)
        kv_results = plain_rows(hidden_rows, kv_cotangent, ranks, rows, True)
        projector_grad = plain_rows(
            cotangent, handoff.reshape(spread * cap, handoff.shape[3]), ranks, rows, False
        )
    return (kv_results[:, :key_cols], kv_results[:, key_cols:], projector_grad, handoff)


def solution(mesh):
    placed = (
        P("dp", None),
        P("dp", "mp"),
        P("dp", "mp"),
        P("dp", None),
        P("dp", None, None, None),
        P(),
        P(),
        P(None, "mp"),
        P("mp"),
        P("mp", None),
        P(),
        P(),
        P("dp", None),
        P("dp", None),
    )
    return jax.shard_map(
        per_device,
        mesh=mesh,
        in_specs=placed,
        out_specs=(P("dp", "mp"), P("dp", "mp"), P("dp", "mp"), P("dp", None, None, "mp")),
        check_vma=False,
    )
```

```python
from functools import partial

import jax
import jax.numpy as jnp
from jax import lax
from jax.experimental import pallas as pl
from jax.experimental.pallas import tpu as pltpu
from jax.sharding import PartitionSpec as P


FEW = 8
CHUNK = 512
ANY = pl.BlockSpec(memory_space=pl.ANY)
VMEM = pl.BlockSpec(memory_space=pltpu.VMEM)
SMEM = pl.BlockSpec(memory_space=pltpu.SMEM)


def shifted(x, axis, by):
    count = lax.axis_size(axis)
    return lax.ppermute(x, axis, [(i, (i + by) % count) for i in range(count)])


def core_swap(x):
    count = lax.axis_size("dp")
    return lax.ppermute(x, "dp", [(i, i ^ 1) for i in range(count)])


def scalar(value):
    return jnp.reshape(value, (1,)).astype(jnp.int32)


def padded(rows):
    return (rows + 15) // 16 * 16


def partial_kernel(core_ref, left_hbm, *refs, parts, ranks, rows, ones_row):
    rights = refs[:parts]
    keep_hbm, send_hbm, left, right_ref, total, stage, in_sem, out_sem = refs[parts:]
    chunks, tokens, chunk = left.shape
    width = chunks * chunk
    stride = stage.shape[1]
    incoming = [
        pltpu.make_async_copy(left_hbm.at[:, pl.ds(c * chunk, chunk)], left.at[c], in_sem.at[c])
        for c in range(chunks)
    ]
    for copy in incoming:
        copy.start()
    if ones_row:
        right = jnp.concatenate([part[...] for part in rights], axis=1)
    else:
        right = jnp.concatenate([part[...] for part in rights], axis=0)
    right_ref[...] = right
    extra = total.shape[0] - width
    if ones_row:
        first = lax.broadcasted_iota(jnp.int32, (extra, tokens), 0) == 0
        picked = jnp.where(first, 1.0, 0.0).astype(jnp.bfloat16)
        total[width:, :] = jnp.dot(picked, right_ref[...], preferred_element_type=jnp.float32)
    else:
        total[width:, :] = jnp.zeros((extra, total.shape[1]), jnp.float32)
    tail = rows // 16 * 16
    if tail < rows:
        for rank in range(ranks):
            stage[rank, tail:, :] = jnp.zeros((stride - tail, total.shape[1]), jnp.bfloat16)

    def outgoing(rank, target):
        place = pl.ds(rank // 2 * stride, stride)
        return pltpu.make_async_copy(stage.at[rank], target.at[place, :], out_sem.at[rank])

    rank = 0
    for c in range(chunks):
        incoming[c].wait()
        total[c * chunk : (c + 1) * chunk, :] = lax.dot_general(
            left[c], right_ref[...], (((0,), (0,)), ((), ())), preferred_element_type=jnp.float32
        )
        ready = (c + 1) * chunk if c + 1 < chunks else ranks * rows
        while rank < ranks and (rank + 1) * rows <= ready:
            stage[rank, :rows, :] = total[rank * rows : (rank + 1) * rows, :].astype(jnp.bfloat16)

            @pl.when(core_ref[0] == rank % 2)
            def _(rank=rank):
                outgoing(rank, keep_hbm).start()

            @pl.when(core_ref[0] != rank % 2)
            def _(rank=rank):
                outgoing(rank, send_hbm).start()

            rank += 1
    for rank in range(ranks):
        outgoing(rank, keep_hbm).wait()


def partial_blocks(left, rights, ranks, rows, ones_row):
    tokens, width = left.shape
    cols = sum(part.shape[1] for part in rights) if ones_row else rights[0].shape[1]
    chunk = CHUNK if width % CHUNK == 0 else width
    stride = padded(rows)
    block = jax.ShapeDtypeStruct((ranks // 2 * stride, cols), jnp.bfloat16)
    return pl.pallas_call(
        partial(partial_kernel, parts=len(rights), ranks=ranks, rows=rows, ones_row=ones_row),
        out_shape=(block, block),
        in_specs=[SMEM, ANY] + [VMEM] * len(rights),
        out_specs=(ANY, ANY),
        scratch_shapes=[
            pltpu.VMEM((width // chunk, tokens, chunk), jnp.bfloat16),
            pltpu.VMEM((tokens, cols), jnp.bfloat16),
            pltpu.VMEM((ranks * rows, cols), jnp.float32),
            pltpu.VMEM((ranks, stride, cols), jnp.bfloat16),
            pltpu.SemaphoreType.DMA((width // chunk,)),
            pltpu.SemaphoreType.DMA((ranks,)),
        ],
        name="partial_kv" if ones_row else "partial_proj",
    )(scalar(lax.axis_index("dp") % 2), left, *rights)


def chip_sum_kernel(chip_ref, keep_hbm, got_hbm, *refs):
    chips = (len(refs) - 5) if len(refs) > 5 else 1
    outs = refs[:chips]
    keep, got, stage, in_sem, out_sem = refs[chips:]
    stride = keep.shape[1]
    rows = outs[0].shape[0]
    order = list(range(1, chips)) + [0]
    copies = {}
    for distance in order:
        target = lax.rem(chip_ref[0] + distance, chips)
        place = pl.ds(pl.multiple_of(target * stride, 16), stride)
        copies[distance] = (
            pltpu.make_async_copy(keep_hbm.at[place, :], keep.at[distance], in_sem.at[distance, 0]),
            pltpu.make_async_copy(got_hbm.at[place, :], got.at[distance], in_sem.at[distance, 1]),
        )
        for copy in copies[distance]:
            copy.start()
    leaving = []
    for distance in order:
        for copy in copies[distance]:
            copy.wait()
        total = keep[distance].astype(jnp.float32) + got[distance].astype(jnp.float32)
        if distance == 0:
            outs[0][...] = total[:rows, :]
        else:
            stage[distance - 1] = total.astype(jnp.bfloat16)
            leaving.append(
                pltpu.make_async_copy(stage.at[distance - 1], outs[distance], out_sem.at[distance - 1])
            )
            leaving[-1].start()
    for copy in leaving:
        copy.wait()


def chip_sums(keep, got, chips, rows):
    stride, cols = keep.shape[0] // chips, keep.shape[1]
    return pl.pallas_call(
        chip_sum_kernel,
        in_specs=[SMEM, ANY, ANY],
        out_specs=(VMEM,) + (ANY,) * (chips - 1),
        out_shape=(jax.ShapeDtypeStruct((rows, cols), jnp.float32),)
        + (jax.ShapeDtypeStruct((stride, cols), jnp.bfloat16),) * (chips - 1),
        scratch_shapes=[
            pltpu.VMEM((chips, stride, cols), jnp.bfloat16),
            pltpu.VMEM((chips, stride, cols), jnp.bfloat16),
            pltpu.VMEM((max(chips - 1, 1), stride, cols), jnp.bfloat16),
            pltpu.SemaphoreType.DMA((chips, 2)),
            pltpu.SemaphoreType.DMA((max(chips - 1, 1),)),
        ],
    )(scalar(lax.axis_index("dp") // 2), keep, got)


def spread_sums(own, sends):
    rows = own.shape[0]
    total = own
    for distance, block in enumerate(sends, 1):
        total = total + shifted(block, "dp", 2 * distance)[:rows].astype(jnp.float32)
    return total


def plain_rows(left, right, ranks, rows, ones_row):
    tokens, width = left.shape
    filler = jnp.zeros((tokens, ranks * rows - width), jnp.bfloat16)
    if ones_row:
        filler = filler.at[:, 0].set(1)
    wide = jnp.concatenate([left, filler], axis=1)
    product = lax.dot_general(wide, right, (((0,), (0,)), ((), ())), preferred_element_type=jnp.float32)
    return lax.psum_scatter(product, "dp", scatter_dimension=0, tiled=True)


def encoder_kernel(
    me_ref, rows_ref, gain_ref, bias_ref, b1_ref, fc1_hbm, fc2_hbm, own_hbm, *refs
):
    sends = refs[:-9]
    fc1, fc2, normed, hidden, own, stage, in1_sem, in2_sem, out_sem = refs[-9:]
    outs = (own_hbm,) + tuple(sends)
    shards = len(outs)
    cols = own.shape[1]
    chunks, _, chunk = fc1.shape
    order = list(range(1, shards)) + [0]
    incoming1 = [
        pltpu.make_async_copy(fc1_hbm.at[:, pl.ds(c * chunk, chunk)], fc1.at[c], in1_sem.at[c])
        for c in range(chunks)
    ]
    incoming2 = []
    for distance in order:
        place = pl.multiple_of(lax.rem(me_ref[0] + distance, shards) * cols, 128)
        incoming2.append(
            pltpu.make_async_copy(
                fc2_hbm.at[:, pl.ds(place, cols)], fc2.at[distance], in2_sem.at[distance]
            )
        )
    for copy in incoming1 + incoming2:
        copy.start()
    values = rows_ref[...].astype(jnp.float32)
    center = jnp.mean(values, axis=1, keepdims=True)
    moved = values - center
    spread_sq = jnp.mean(moved * moved, axis=1, keepdims=True)
    normed[...] = (moved * lax.rsqrt(spread_sq + 1e-06) * gain_ref[...] + bias_ref[...]).astype(
        jnp.bfloat16
    )
    for c in range(chunks):
        incoming1[c].wait()
        part = slice(c * chunk, (c + 1) * chunk)
        before = jnp.dot(normed[...], fc1[c], preferred_element_type=jnp.float32) + b1_ref[:, part]
        hidden[:, part] = (0.5 * before * (1.0 + lax.erf(before * 0.7071067811865476))).astype(
            jnp.bfloat16
        )
    leaving = []
    for distance, copy in zip(order, incoming2):
        copy.wait()
        total = jnp.dot(hidden[...], fc2[distance], preferred_element_type=jnp.float32)
        if distance == 0:
            own[...] = total
            source = own
        else:
            stage[distance] = total.astype(jnp.bfloat16)
            source = stage.at[distance]
        leaving.append(pltpu.make_async_copy(source, outs[distance], out_sem.at[distance]))
        leaving[-1].start()
    for copy in leaving:
        copy.wait()


def encoder_partials(rows, gain, bias, fc1, b1, fc2):
    shards = lax.axis_size("mp")
    count, feats = rows.shape
    units = fc1.shape[1]
    chunk = 256 if units % 256 == 0 else units
    cols = feats // shards
    return pl.pallas_call(
        encoder_kernel,
        out_shape=(jax.ShapeDtypeStruct((count, cols), jnp.float32),)
        + (jax.ShapeDtypeStruct((count, cols), jnp.bfloat16),) * (shards - 1),
        in_specs=[SMEM, VMEM, VMEM, VMEM, VMEM, ANY, ANY],
        out_specs=(ANY,) * shards,
        scratch_shapes=[
            pltpu.VMEM((units // chunk, feats, chunk), jnp.bfloat16),
            pltpu.VMEM((shards, units, cols), jnp.bfloat16),
            pltpu.VMEM((count, feats), jnp.bfloat16),
            pltpu.VMEM((count, units), jnp.bfloat16),
            pltpu.VMEM((count, cols), jnp.float32),
            pltpu.VMEM((shards, count, cols), jnp.bfloat16),
            pltpu.SemaphoreType.DMA((units // chunk,)),
            pltpu.SemaphoreType.DMA((shards,)),
            pltpu.SemaphoreType.DMA((shards,)),
        ],
        name="encoder",
    )(scalar(lax.axis_index("mp")), rows, gain[None], bias[None], b1[None], fc1, fc2)


def pack_kernel(me_ref, counts_ref, offsets_ref, rows_ref, scale_ref, bias_ref, own_ref, *refs, spread):
    parts, outs = refs[:-spread], refs[-spread:]
    images = counts_ref.shape[0]
    cap = outs[0].shape[0]
    total_rows = rows_ref.shape[0]
    summed = own_ref[...]
    for part in parts:
        summed = summed + part[...].astype(jnp.float32)
    encoded = rows_ref[...].astype(jnp.float32) + scale_ref[...] * (summed + bias_ref[...])
    encoded = encoded.astype(jnp.bfloat16)
    place = lax.broadcasted_iota(jnp.int32, (1, total_rows), 1)
    target = jnp.full((1, total_rows), -1, jnp.int32)
    start = jnp.int32(0)
    for image in range(images):
        count, offset = counts_ref[image], offsets_ref[image]
        before = jnp.int32(0)
        for other in range(image):
            before = before + jnp.where(offsets_ref[other] == offset, counts_ref[other], 0)
        inside = (place >= start) & (place < start + count)
        target = jnp.where(inside, place + ((offset - 1) * cap + before - start), target)
        start = start + count
    slot = lax.broadcasted_iota(jnp.int32, (spread * cap, total_rows), 0)
    select = jnp.where(slot == target, 1.0, 0.0).astype(jnp.bfloat16)
    packed = jnp.dot(select, encoded, preferred_element_type=jnp.float32).astype(jnp.bfloat16)
    for distance in range(spread):
        outs[distance][...] = packed[distance * cap : (distance + 1) * cap, :]


def packed_rows(rows, scale, bias, own, parts, counts, offsets, spread, cap):
    count, cols = own.shape
    line = pl.BlockSpec((1, cols), lambda i, m, c, o: (0, m[0]))
    whole = pl.BlockSpec((count, cols), lambda i, m, c, o: (0, 0))
    return pl.pallas_call(
        partial(pack_kernel, spread=spread),
        out_shape=(jax.ShapeDtypeStruct((cap, cols), jnp.bfloat16),) * spread,
        grid_spec=pltpu.PrefetchScalarGridSpec(
            num_scalar_prefetch=3,
            grid=(1,),
            in_specs=[pl.BlockSpec((count, cols), lambda i, m, c, o: (0, m[0])), line, line]
            + [whole] * (1 + len(parts)),
            out_specs=(pl.BlockSpec((cap, cols), lambda i, m, c, o: (0, 0)),) * spread,
        ),
        name="pack",
    )(scalar(lax.axis_index("mp")), counts, offsets, rows, scale[None], bias[None], own, *parts)


def bucket(
    hidden_rows,
    key_grad,
    value_grad,
    visual_rows,
    visual_cotangent,
    norm_gain,
    norm_bias,
    fc1_weight,
    fc1_bias,
    fc2_weight,
    fc2_bias,
    layer_scale,
    token_counts,
    dest_offsets,
):
    width = hidden_rows.shape[1]
    ranks = lax.axis_size("dp")
    rows = (width + ranks) // ranks
    spread, cap = visual_cotangent.shape[1:3]
    key_cols = key_grad.shape[1]
    stepped = ranks <= FEW and ranks % 2 == 0
    chips = ranks // 2

    own, *sends = encoder_partials(
        visual_rows, norm_gain, norm_bias, fc1_weight, fc1_bias, fc2_weight
    )
    parts = [shifted(block, "mp", distance) for distance, block in enumerate(sends, 1)]
    if stepped:
        left, own = lax.optimization_barrier((hidden_rows, own))
        kv_keep, kv_send = partial_blocks(left, (key_grad, value_grad), ranks, rows, True)
        kv_got = core_swap(kv_send)
        own, kv_keep = lax.optimization_barrier((own, kv_keep))
    packed = packed_rows(
        visual_rows,
        layer_scale,
        fc2_bias,
        own,
        parts,
        token_counts[0],
        dest_offsets[0],
        spread,
        cap,
    )
    if stepped:
        packed, kv_keep = lax.optimization_barrier((packed, kv_keep))
    received = [shifted(block, "dp", distance) for distance, block in enumerate(packed, 1)]
    handoff = jnp.stack(received, axis=0)[None]
    cotangent = visual_cotangent.reshape(spread * cap, width)
    if stepped:
        kv_own, *kv_sends = chip_sums(kv_keep, kv_got, chips, rows)
        cotangent, kv_own = lax.optimization_barrier((cotangent, kv_own))
        keep, send = partial_blocks(cotangent, received, ranks, rows, False)
        got = core_swap(send)
        kv_results = spread_sums(kv_own, kv_sends)
        proj_own, *proj_sends = chip_sums(keep, got, chips, rows)
        projector_grad = spread_sums(proj_own, proj_sends)
    else:
        kv_cotangent = jnp.concatenate([key_grad, value_grad], axis=1)
        kv_results = plain_rows(hidden_rows, kv_cotangent, ranks, rows, True)
        projector_grad = plain_rows(
            cotangent, handoff.reshape(spread * cap, handoff.shape[3]), ranks, rows, False
        )
    return (kv_results[:, :key_cols], kv_results[:, key_cols:], projector_grad, handoff)


def solution(mesh):
    placed = (
        P("dp", None),
        P("dp", "mp"),
        P("dp", "mp"),
        P("dp", None),
        P("dp", None, None, None),
        P(),
        P(),
        P(None, "mp"),
        P("mp"),
        P("mp", None),
        P(),
        P(),
        P("dp", None),
        P("dp", None),
    )
    return jax.shard_map(
        bucket,
        mesh=mesh,
        in_specs=placed,
        out_specs=(P("dp", "mp"), P("dp", "mp"), P("dp", "mp"), P("dp", None, None, "mp")),
        check_vma=False,
    )
```

```python
from functools import partial

import jax
import jax.numpy as jnp
from jax import lax
from jax.experimental import pallas as pl
from jax.experimental.pallas import tpu as pltpu
from jax.sharding import PartitionSpec as P


FEW = 8
CHUNK = 512
ANY = pl.BlockSpec(memory_space=pl.ANY)
VMEM = pl.BlockSpec(memory_space=pltpu.VMEM)
SMEM = pl.BlockSpec(memory_space=pltpu.SMEM)


def shifted(x, axis, by):
    count = lax.axis_size(axis)
    return lax.ppermute(x, axis, [(i, (i + by) % count) for i in range(count)])


def core_swap(x):
    count = lax.axis_size("dp")
    return lax.ppermute(x, "dp", [(i, i ^ 1) for i in range(count)])


def scalar(value):
    return jnp.reshape(value, (1,)).astype(jnp.int32)


def padded(rows):
    return (rows + 15) // 16 * 16


def partial_kernel(core_ref, left_hbm, *refs, parts, ranks, rows, ones_row):
    rights = refs[:parts]
    keep_hbm, send_hbm, left, right_ref, total, stage, in_sem, out_sem = refs[parts:]
    chunks, tokens, chunk = left.shape
    width = chunks * chunk
    stride = stage.shape[1]
    incoming = [
        pltpu.make_async_copy(left_hbm.at[:, pl.ds(c * chunk, chunk)], left.at[c], in_sem.at[c])
        for c in range(chunks)
    ]
    for copy in incoming:
        copy.start()
    if ones_row:
        right = jnp.concatenate([part[...] for part in rights], axis=1)
    else:
        right = jnp.concatenate([part[...] for part in rights], axis=0)
    right_ref[...] = right
    extra = total.shape[0] - width
    if ones_row:
        first = lax.broadcasted_iota(jnp.int32, (extra, tokens), 0) == 0
        picked = jnp.where(first, 1.0, 0.0).astype(jnp.bfloat16)
        total[width:, :] = jnp.dot(picked, right_ref[...], preferred_element_type=jnp.float32)
    else:
        total[width:, :] = jnp.zeros((extra, total.shape[1]), jnp.float32)
    tail = rows // 16 * 16
    if tail < rows:
        for rank in range(ranks):
            stage[rank, tail:, :] = jnp.zeros((stride - tail, total.shape[1]), jnp.bfloat16)

    def outgoing(rank, target):
        place = pl.ds(rank // 2 * stride, stride)
        return pltpu.make_async_copy(stage.at[rank], target.at[place, :], out_sem.at[rank])

    rank = 0
    for c in range(chunks):
        incoming[c].wait()
        total[c * chunk : (c + 1) * chunk, :] = lax.dot_general(
            left[c], right_ref[...], (((0,), (0,)), ((), ())), preferred_element_type=jnp.float32
        )
        ready = (c + 1) * chunk if c + 1 < chunks else ranks * rows
        while rank < ranks and (rank + 1) * rows <= ready:
            stage[rank, :rows, :] = total[rank * rows : (rank + 1) * rows, :].astype(jnp.bfloat16)

            @pl.when(core_ref[0] == rank % 2)
            def _(rank=rank):
                outgoing(rank, keep_hbm).start()

            @pl.when(core_ref[0] != rank % 2)
            def _(rank=rank):
                outgoing(rank, send_hbm).start()

            rank += 1
    for rank in range(ranks):
        outgoing(rank, keep_hbm).wait()


def partial_blocks(left, rights, ranks, rows, ones_row):
    tokens, width = left.shape
    cols = sum(part.shape[1] for part in rights) if ones_row else rights[0].shape[1]
    chunk = CHUNK if width % CHUNK == 0 else width
    stride = padded(rows)
    block = jax.ShapeDtypeStruct((ranks // 2 * stride, cols), jnp.bfloat16)
    return pl.pallas_call(
        partial(partial_kernel, parts=len(rights), ranks=ranks, rows=rows, ones_row=ones_row),
        out_shape=(block, block),
        in_specs=[SMEM, ANY] + [VMEM] * len(rights),
        out_specs=(ANY, ANY),
        scratch_shapes=[
            pltpu.VMEM((width // chunk, tokens, chunk), jnp.bfloat16),
            pltpu.VMEM((tokens, cols), jnp.bfloat16),
            pltpu.VMEM((ranks * rows, cols), jnp.float32),
            pltpu.VMEM((ranks, stride, cols), jnp.bfloat16),
            pltpu.SemaphoreType.DMA((width // chunk,)),
            pltpu.SemaphoreType.DMA((ranks,)),
        ],
        name="partial_kv" if ones_row else "partial_proj",
    )(scalar(lax.axis_index("dp") % 2), left, *rights)


def chip_sum_kernel(chip_ref, keep_hbm, got_hbm, *refs):
    chips = (len(refs) - 5) if len(refs) > 5 else 1
    outs = refs[:chips]
    keep, got, stage, in_sem, out_sem = refs[chips:]
    stride = keep.shape[1]
    rows = outs[0].shape[0]
    order = list(range(1, chips)) + [0]
    copies = {}
    for distance in order:
        target = lax.rem(chip_ref[0] + distance, chips)
        place = pl.ds(pl.multiple_of(target * stride, 16), stride)
        copies[distance] = (
            pltpu.make_async_copy(keep_hbm.at[place, :], keep.at[distance], in_sem.at[distance, 0]),
            pltpu.make_async_copy(got_hbm.at[place, :], got.at[distance], in_sem.at[distance, 1]),
        )
        for copy in copies[distance]:
            copy.start()
    leaving = []
    for distance in order:
        for copy in copies[distance]:
            copy.wait()
        total = keep[distance].astype(jnp.float32) + got[distance].astype(jnp.float32)
        if distance == 0:
            outs[0][...] = total[:rows, :]
        else:
            stage[distance - 1] = total.astype(jnp.bfloat16)
            leaving.append(
                pltpu.make_async_copy(stage.at[distance - 1], outs[distance], out_sem.at[distance - 1])
            )
            leaving[-1].start()
    for copy in leaving:
        copy.wait()


def chip_sums(keep, got, chips, rows):
    stride, cols = keep.shape[0] // chips, keep.shape[1]
    return pl.pallas_call(
        chip_sum_kernel,
        in_specs=[SMEM, ANY, ANY],
        out_specs=(VMEM,) + (ANY,) * (chips - 1),
        out_shape=(jax.ShapeDtypeStruct((rows, cols), jnp.float32),)
        + (jax.ShapeDtypeStruct((stride, cols), jnp.bfloat16),) * (chips - 1),
        scratch_shapes=[
            pltpu.VMEM((chips, stride, cols), jnp.bfloat16),
            pltpu.VMEM((chips, stride, cols), jnp.bfloat16),
            pltpu.VMEM((max(chips - 1, 1), stride, cols), jnp.bfloat16),
            pltpu.SemaphoreType.DMA((chips, 2)),
            pltpu.SemaphoreType.DMA((max(chips - 1, 1),)),
        ],
    )(scalar(lax.axis_index("dp") // 2), keep, got)


def spread_sums(own, sends):
    rows = own.shape[0]
    total = own
    for distance, block in enumerate(sends, 1):
        total = total + shifted(block, "dp", 2 * distance)[:rows].astype(jnp.float32)
    return total


def plain_rows(left, right, ranks, rows, ones_row):
    tokens, width = left.shape
    filler = jnp.zeros((tokens, ranks * rows - width), jnp.bfloat16)
    if ones_row:
        filler = filler.at[:, 0].set(1)
    wide = jnp.concatenate([left, filler], axis=1)
    product = lax.dot_general(wide, right, (((0,), (0,)), ((), ())), preferred_element_type=jnp.float32)
    return lax.psum_scatter(product, "dp", scatter_dimension=0, tiled=True)


def encoder_kernel(
    me_ref, rows_ref, gain_ref, bias_ref, b1_ref, fc1_hbm, fc2_hbm, own_hbm, *refs
):
    sends = refs[:-9]
    fc1, fc2, normed, hidden, own, stage, in1_sem, in2_sem, out_sem = refs[-9:]
    outs = (own_hbm,) + tuple(sends)
    shards = len(outs)
    cols = own.shape[1]
    chunks, _, chunk = fc1.shape
    order = list(range(1, shards)) + [0]
    incoming1 = [
        pltpu.make_async_copy(fc1_hbm.at[:, pl.ds(c * chunk, chunk)], fc1.at[c], in1_sem.at[c])
        for c in range(chunks)
    ]
    incoming2 = []
    for distance in order:
        place = pl.multiple_of(lax.rem(me_ref[0] + distance, shards) * cols, 128)
        incoming2.append(
            pltpu.make_async_copy(
                fc2_hbm.at[:, pl.ds(place, cols)], fc2.at[distance], in2_sem.at[distance]
            )
        )
    for copy in incoming1 + incoming2:
        copy.start()
    values = rows_ref[...].astype(jnp.float32)
    center = jnp.mean(values, axis=1, keepdims=True)
    moved = values - center
    spread_sq = jnp.mean(moved * moved, axis=1, keepdims=True)
    normed[...] = (moved * lax.rsqrt(spread_sq + 1e-06) * gain_ref[...] + bias_ref[...]).astype(
        jnp.bfloat16
    )
    for c in range(chunks):
        incoming1[c].wait()
        part = slice(c * chunk, (c + 1) * chunk)
        before = jnp.dot(normed[...], fc1[c], preferred_element_type=jnp.float32) + b1_ref[:, part]
        hidden[:, part] = (0.5 * before * (1.0 + lax.erf(before * 0.7071067811865476))).astype(
            jnp.bfloat16
        )
    leaving = []
    for distance, copy in zip(order, incoming2):
        copy.wait()
        total = jnp.dot(hidden[...], fc2[distance], preferred_element_type=jnp.float32)
        if distance == 0:
            own[...] = total
            source = own
        else:
            stage[distance] = total.astype(jnp.bfloat16)
            source = stage.at[distance]
        leaving.append(pltpu.make_async_copy(source, outs[distance], out_sem.at[distance]))
        leaving[-1].start()
    for copy in leaving:
        copy.wait()


def encoder_partials(rows, gain, bias, fc1, b1, fc2):
    shards = lax.axis_size("mp")
    count, feats = rows.shape
    units = fc1.shape[1]
    chunk = 256 if units % 256 == 0 else units
    cols = feats // shards
    return pl.pallas_call(
        encoder_kernel,
        out_shape=(jax.ShapeDtypeStruct((count, cols), jnp.float32),)
        + (jax.ShapeDtypeStruct((count, cols), jnp.bfloat16),) * (shards - 1),
        in_specs=[SMEM, VMEM, VMEM, VMEM, VMEM, ANY, ANY],
        out_specs=(ANY,) * shards,
        scratch_shapes=[
            pltpu.VMEM((units // chunk, feats, chunk), jnp.bfloat16),
            pltpu.VMEM((shards, units, cols), jnp.bfloat16),
            pltpu.VMEM((count, feats), jnp.bfloat16),
            pltpu.VMEM((count, units), jnp.bfloat16),
            pltpu.VMEM((count, cols), jnp.float32),
            pltpu.VMEM((shards, count, cols), jnp.bfloat16),
            pltpu.SemaphoreType.DMA((units // chunk,)),
            pltpu.SemaphoreType.DMA((shards,)),
            pltpu.SemaphoreType.DMA((shards,)),
        ],
        name="encoder",
    )(scalar(lax.axis_index("mp")), rows, gain[None], bias[None], b1[None], fc1, fc2)


def pack_kernel(me_ref, counts_ref, offsets_ref, rows_ref, scale_ref, bias_ref, own_ref, *refs, spread):
    parts, outs = refs[:-spread], refs[-spread:]
    images = counts_ref.shape[0]
    cap = outs[0].shape[0]
    total_rows = rows_ref.shape[0]
    summed = own_ref[...]
    for part in parts:
        summed = summed + part[...].astype(jnp.float32)
    encoded = rows_ref[...].astype(jnp.float32) + scale_ref[...] * (summed + bias_ref[...])
    encoded = encoded.astype(jnp.bfloat16)
    place = lax.broadcasted_iota(jnp.int32, (1, total_rows), 1)
    target = jnp.full((1, total_rows), -1, jnp.int32)
    start = jnp.int32(0)
    for image in range(images):
        count, offset = counts_ref[image], offsets_ref[image]
        before = jnp.int32(0)
        for other in range(image):
            before = before + jnp.where(offsets_ref[other] == offset, counts_ref[other], 0)
        inside = (place >= start) & (place < start + count)
        target = jnp.where(inside, place + ((offset - 1) * cap + before - start), target)
        start = start + count
    slot = lax.broadcasted_iota(jnp.int32, (spread * cap, total_rows), 0)
    select = jnp.where(slot == target, 1.0, 0.0).astype(jnp.bfloat16)
    packed = jnp.dot(select, encoded, preferred_element_type=jnp.float32).astype(jnp.bfloat16)
    for distance in range(spread):
        outs[distance][...] = packed[distance * cap : (distance + 1) * cap, :]


def packed_rows(rows, scale, bias, own, parts, counts, offsets, spread, cap):
    count, cols = own.shape
    line = pl.BlockSpec((1, cols), lambda i, m, c, o: (0, m[0]))
    whole = pl.BlockSpec((count, cols), lambda i, m, c, o: (0, 0))
    return pl.pallas_call(
        partial(pack_kernel, spread=spread),
        out_shape=(jax.ShapeDtypeStruct((cap, cols), jnp.bfloat16),) * spread,
        grid_spec=pltpu.PrefetchScalarGridSpec(
            num_scalar_prefetch=3,
            grid=(1,),
            in_specs=[pl.BlockSpec((count, cols), lambda i, m, c, o: (0, m[0])), line, line]
            + [whole] * (1 + len(parts)),
            out_specs=(pl.BlockSpec((cap, cols), lambda i, m, c, o: (0, 0)),) * spread,
        ),
        name="pack",
    )(scalar(lax.axis_index("mp")), counts, offsets, rows, scale[None], bias[None], own, *parts)


def bucket(
    hidden_rows,
    key_grad,
    value_grad,
    visual_rows,
    visual_cotangent,
    norm_gain,
    norm_bias,
    fc1_weight,
    fc1_bias,
    fc2_weight,
    fc2_bias,
    layer_scale,
    token_counts,
    dest_offsets,
):
    width = hidden_rows.shape[1]
    ranks = lax.axis_size("dp")
    rows = (width + ranks) // ranks
    spread, cap = visual_cotangent.shape[1:3]
    key_cols = key_grad.shape[1]
    stepped = ranks <= FEW and ranks % 2 == 0
    chips = ranks // 2

    first_rows = visual_rows
    if stepped:
        kv_keep, kv_send = partial_blocks(hidden_rows, (key_grad, value_grad), ranks, rows, True)
        kv_got = core_swap(kv_send)
        first_rows, kv_keep = lax.optimization_barrier((first_rows, kv_keep))
    own, *sends = encoder_partials(
        first_rows, norm_gain, norm_bias, fc1_weight, fc1_bias, fc2_weight
    )
    parts = [shifted(block, "mp", distance) for distance, block in enumerate(sends, 1)]
    if stepped:
        own, kv_keep = lax.optimization_barrier((own, kv_keep))
        kv_own, *kv_sends = chip_sums(kv_keep, kv_got, chips, rows)
        own, kv_own = lax.optimization_barrier((own, kv_own))
    packed = packed_rows(
        visual_rows,
        layer_scale,
        fc2_bias,
        own,
        parts,
        token_counts[0],
        dest_offsets[0],
        spread,
        cap,
    )
    received = [shifted(block, "dp", distance) for distance, block in enumerate(packed, 1)]
    handoff = jnp.stack(received, axis=0)[None]
    cotangent = visual_cotangent.reshape(spread * cap, width)
    if stepped:
        keep, send = partial_blocks(cotangent, received, ranks, rows, False)
        got = core_swap(send)
        kv_results = spread_sums(kv_own, kv_sends)
        proj_own, *proj_sends = chip_sums(keep, got, chips, rows)
        projector_grad = spread_sums(proj_own, proj_sends)
    else:
        kv_cotangent = jnp.concatenate([key_grad, value_grad], axis=1)
        kv_results = plain_rows(hidden_rows, kv_cotangent, ranks, rows, True)
        projector_grad = plain_rows(
            cotangent, handoff.reshape(spread * cap, handoff.shape[3]), ranks, rows, False
        )
    return (kv_results[:, :key_cols], kv_results[:, key_cols:], projector_grad, handoff)


def solution(mesh):
    placed = (
        P("dp", None),
        P("dp", "mp"),
        P("dp", "mp"),
        P("dp", None),
        P("dp", None, None, None),
        P(),
        P(),
        P(None, "mp"),
        P("mp"),
        P("mp", None),
        P(),
        P(),
        P("dp", None),
        P("dp", None),
    )
    return jax.shard_map(
        bucket,
        mesh=mesh,
        in_specs=placed,
        out_specs=(P("dp", "mp"), P("dp", "mp"), P("dp", "mp"), P("dp", None, None, "mp")),
        check_vma=False,
    )
```
